1024 devices in a mesh: img: 64 (over x_hi, y, core), txt: 16 (over x_lo, z).
Axes of the slice: x: 8 (x_hi: 4, x_lo: 2; x = x_hi * 2 + x_lo), y: 8, z: 8, core: 2. Of those that a mesh axis runs over, the one named last changes fastest.
Arguments:
- images: bfloat16 [24576, 512], P('img'), may hold values from -1 to 1
- texts: bfloat16 [24576, 512], P(('txt', 'img')), may hold values from -1 to 1
Outputs:
- grad_images: float32 [24576, 512], P(('img', 'txt'))
- grad_texts: float32 [24576, 512], P(('txt', 'img'))
The draws below stay inside these ranges and needn't reach their ends.
All inputs are finite; a program needn't handle non-finite values.
Results may differ from the reference program's by a relative error of at most 0.0075.
Values may be sent and summed in bfloat16 or wider, within the bound.
No kernel may reach another device: no remote copies, remote signals or barrier semaphores. Data moves between devices by JAX's collectives and lax.ppermute only.
A program may use at most 32 MiB of HBM per device.

```python
import math
import jax
import jax.numpy as jnp
from jax import lax

D = 512
ROUNDS = 3
NPAIR = 24576


cluster_count = 16


noise_scale = 0.05


def rough_draw(key, shape):
    return jax.random.truncated_normal(key, -4.0, 4.0, shape, jnp.float32)


def shared_parts(key):
    shared_key = jax.random.fold_in(key, 11)
    k_group, k_center, k_noise, k_imgamp, k_txtamp = jax.random.split(shared_key, 5)
    groups = jax.random.randint(k_group, (NPAIR,), 0, cluster_count)
    centers = noise_scale * rough_draw(k_center, (cluster_count, D))
    shared_center = jnp.take(centers, groups, axis=0)
    img_noise = noise_scale * rough_draw(k_noise, (NPAIR, D))
    lowest_amp = 0.3
    img_amp = jax.random.uniform(k_imgamp, (NPAIR, 1), jnp.float32, lowest_amp, 3.0)
    txt_amp = jax.random.uniform(k_txtamp, (NPAIR, 1), jnp.float32, lowest_amp, 3.0)
    return (shared_center, img_noise, img_amp, txt_amp)


def draw_images(key, part):
    shared_center, img_noise, img_amp, txt_amp = shared_parts(key)
    values = img_amp * shared_center + img_noise
    return values.astype(jnp.bfloat16)


def draw_texts(key, part):
    shared_center, img_noise, img_amp, txt_amp = shared_parts(key)
    own_noise = noise_scale * rough_draw(jax.random.fold_in(key, 31), (NPAIR, D))
    values = txt_amp * shared_center + 0.6 * img_noise + 0.8 * own_noise
    return values.astype(jnp.bfloat16)


def setup_inputs(seed: int = 0) -> dict:
    arg_keys = jax.random.split(jax.random.key(seed), 3)
    images = draw_images(jax.random.fold_in(arg_keys[2], 71), 0)
    texts = draw_texts(jax.random.fold_in(arg_keys[2], 71), 0)
    return {"images": images, "texts": texts}


logit_scale = 30.0
mix_weight = 0.5
norm_eps = 1e-06
highest = lax.Precision.HIGHEST

def normalize(values):
    wide = values.astype(jnp.float32)
    length = jnp.sqrt(lax.optimization_barrier(jnp.sum(wide * wide, axis=1, keepdims=True)) + norm_eps)
    return (wide / length, length)

def project_back(grad, unit, length):
    along = lax.optimization_barrier(jnp.sum(unit * grad, axis=1, keepdims=True))
    return (grad - unit * along) / length

def reference(images, texts):
    unit_img, len_img = normalize(images)
    unit_txt, len_txt = normalize(texts)
    img_wide = unit_img.astype(jnp.bfloat16).astype(jnp.float32)
    txt_wide = unit_txt.astype(jnp.bfloat16).astype(jnp.float32)
    total = float(NPAIR)
    block = math.gcd(512, NPAIR)
    count = NPAIR // block
    starts = jnp.arange(count, dtype=jnp.int32) * block

    def kernel_rows(start):
        rows = lax.dynamic_slice_in_dim(img_wide, start, block, 0)
        scores = logit_scale * jnp.dot(rows, txt_wide.T, precision=highest, preferred_element_type=jnp.float32)
        return (rows, jnp.exp(scores - logit_scale))

    def first_pass(carry, start):
        rows, kernel = kernel_rows(start)
        return (carry + lax.optimization_barrier(jnp.sum(kernel, axis=0)), lax.optimization_barrier(jnp.sum(kernel, axis=1)))
    col_total, row_parts = lax.scan(first_pass, jnp.zeros((NPAIR,), jnp.float32), starts)
    row_total = row_parts.reshape(NPAIR)
    col_vec = col_total
    row_weight = jnp.ones((NPAIR,), jnp.float32)
    col_scale = jnp.ones((NPAIR,), jnp.float32)
    for step in range(ROUNDS):
        col_scale = 1.0 / (total * col_vec)

        def round_pass(carry, start, col_scale=col_scale):
            rows, kernel = kernel_rows(start)
            row_sum = jnp.dot(kernel, col_scale, precision=highest)
            weight = 1.0 / (total * row_sum)
            return (carry + jnp.dot(weight, kernel, precision=highest), weight)
        col_vec, weights = lax.scan(round_pass, jnp.zeros((NPAIR,), jnp.float32), starts)
        row_weight = weights.reshape(NPAIR)
    col_weight = 1.0 - mix_weight + mix_weight * total * col_scale * col_vec
    txt_ids = jnp.arange(NPAIR, dtype=jnp.int32)

    def grad_pass(carry, start):
        rows, kernel = kernel_rows(start)
        img_ids = start + jnp.arange(block, dtype=jnp.int32)
        eye = (img_ids[:, None] == txt_ids[None, :]).astype(jnp.float32)
        weight = lax.dynamic_slice_in_dim(row_weight, start, block, 0)
        rtot = lax.dynamic_slice_in_dim(row_total, start, block, 0)
        target = (1.0 - mix_weight) * eye + mix_weight * total * weight[:, None] * kernel * col_scale[None, :]
        grad_logit = 0.5 * (kernel / rtot[:, None] + col_weight[None, :] * kernel / col_total[None, :] - 2.0 * target)
        grad_wide = grad_logit.astype(jnp.bfloat16).astype(jnp.float32)
        g_rows = logit_scale * jnp.dot(grad_wide, txt_wide, precision=highest)
        g_cols = logit_scale * jnp.dot(grad_wide.T, rows, precision=highest)
        return (carry + g_cols, g_rows)
    g_txt, g_parts = lax.scan(grad_pass, jnp.zeros((NPAIR, D), jnp.float32), starts)
    g_img = g_parts.reshape(NPAIR, D)
    return (project_back(g_img, unit_img, len_img), project_back(g_txt, unit_txt, len_txt))
```

```python
import jax
import jax.numpy as jnp
from jax import lax
from jax.sharding import Mesh, PartitionSpec as P

ROUNDS = 3
CORES = 2

logit_scale = 30.0
mix_weight = 0.5
norm_eps = 1e-06


def normalize(values):
    wide = values.astype(jnp.float32)
    length = jnp.sqrt(jnp.sum(wide * wide, axis=1, keepdims=True) + norm_eps)
    return (wide / length, length)


def project_back(grad, unit, length):
    along = jnp.sum(unit * grad, axis=1, keepdims=True)
    return (grad - unit * along) / length


def share(values, axes):
    count = lax.axis_size(axes)
    copies = jnp.broadcast_to(values[None], (count,) + values.shape)
    return lax.all_to_all(copies, axes, 0, 0, tiled=True)


def total_over(values, axes):
    return jnp.sum(share(values, axes), axis=0)


def scatter_sum(values, axes):
    count = lax.axis_size(axes)
    parts = values.astype(jnp.bfloat16).reshape(count, -1, values.shape[1])
    return jnp.sum(lax.all_to_all(parts, axes, 0, 0, tiled=True).astype(jnp.float32), axis=0)


def shards(images, texts):
    own = texts.shape[0]
    p_index = lax.axis_index("p")
    c_index = lax.axis_index("c")
    t_index = lax.axis_index("t")
    unit_txt, len_txt = normalize(texts)
    txt_bf = share(unit_txt.astype(jnp.bfloat16), "p").reshape(-1, texts.shape[1])
    both = lax.all_gather(images, "c", axis=0, tiled=True)
    unit_img, len_img = normalize(both)
    img_bf = unit_img.astype(jnp.bfloat16)
    n_img, n_txt = img_bf.shape[0], txt_bf.shape[0]
    total = float(n_img * lax.axis_size("p"))
    scores = logit_scale * lax.dot_general(
        img_bf, txt_bf, (((1,), (1,)), ((), ())), preferred_element_type=jnp.float32
    )
    kernel = jnp.exp(scores - logit_scale)
    col_total = total_over(jnp.sum(kernel, axis=0), "p")
    col_sum = col_total
    for step in range(ROUNDS):
        col_scale = 1.0 / (total * col_sum)
        row_part = jnp.sum(kernel * col_scale[None, :], axis=1)
        if step == 0:
            stats = total_over(jnp.stack([row_part, jnp.sum(kernel, axis=1)]), ("c", "t"))
            row_sum, row_total = stats[0], stats[1]
        else:
            row_sum = total_over(row_part, ("c", "t"))
        row_weight = 1.0 / (total * row_sum)
        col_sum = total_over(jnp.sum(kernel * row_weight[:, None], axis=0), "p")
    col_weight = 1.0 - mix_weight + mix_weight * total * col_scale * col_sum
    img_ids = p_index * n_img + jnp.arange(n_img, dtype=jnp.int32)
    place = jnp.arange(n_txt, dtype=jnp.int32)
    txt_ids = t_index * (n_txt * CORES) + (place // own * CORES + c_index) * own + place % own
    eye = (img_ids[:, None] == txt_ids[None, :]).astype(jnp.float32)
    target = (1.0 - mix_weight) * eye + mix_weight * total * row_weight[
        :, None
    ] * kernel * col_scale[None, :]
    grad_logit = 0.5 * (
        kernel / row_total[:, None]
        + col_weight[None, :] * kernel / col_total[None, :]
        - 2.0 * target
    )
    grad_logit = grad_logit.astype(jnp.bfloat16)
    g_img = scatter_sum(
        logit_scale * jnp.dot(grad_logit, txt_bf, preferred_element_type=jnp.float32), ("c", "t")
    )
    g_txt = scatter_sum(
        logit_scale
        * lax.dot_general(
            grad_logit, img_bf, (((0,), (0,)), ((), ())), preferred_element_type=jnp.float32
        ),
        "p",
    )
    first = c_index * (n_img // CORES) + t_index * own
    own_unit = lax.dynamic_slice_in_dim(unit_img, first, own, 0)
    own_len = lax.dynamic_slice_in_dim(len_img, first, own, 0)
    grad_images = project_back(g_img, own_unit, own_len)
    grad_texts = project_back(g_txt, unit_txt, len_txt)
    return (grad_images, grad_texts)


def solution(mesh):
    n_img, n_txt = mesh.devices.shape
    split = Mesh(mesh.devices.reshape(n_img // CORES, CORES, n_txt), ("p", "c", "t"))
    return jax.shard_map(
        shards,
        mesh=split,
        in_specs=(P(("p", "c"), None), P(("t", "p", "c"), None)),
        out_specs=(P(("p", "c", "t"), None), P(("t", "p", "c"), None)),
        check_vma=False,
    )
```

```python
import jax
import jax.numpy as jnp
from jax import lax
from jax.sharding import Mesh, PartitionSpec as P

ROUNDS = 3
CORES = 2
NEAR = 2
FAR = 2

logit_scale = 30.0
mix_weight = 0.5
norm_eps = 1e-06


def normalize(values):
    wide = values.astype(jnp.float32)
    length = jnp.sqrt(jnp.sum(wide * wide, axis=1, keepdims=True) + norm_eps)
    return (wide / length, length)


def project_back(grad, unit, length):
    along = jnp.sum(unit * grad, axis=1, keepdims=True)
    return (grad - unit * along) / length


def exchange(parts, axes):
    return lax.all_to_all(parts, axes, 0, 0, tiled=True)


def share(values, axes):
    return exchange(jnp.broadcast_to(values[None], (lax.axis_size(axes),) + values.shape), axes)


def total_over(values, axes):
    return jnp.sum(share(values, axes), axis=0)


def scatter_sum(values, axes):
    return jnp.sum(exchange(values.astype(jnp.bfloat16), axes).astype(jnp.float32), axis=0)


def keep_half(values, axis, dim, dtype):
    me = lax.axis_index(axis)
    half = values.shape[dim] // 2
    mine = lax.dynamic_slice_in_dim(values, me * half, half, dim)
    other = lax.dynamic_slice_in_dim(values, (1 - me) * half, half, dim)
    return mine + lax.ppermute(other.astype(dtype), axis, [(0, 1), (1, 0)]).astype(jnp.float32)


def shards(images, texts):
    own, width = texts.shape
    p_index = lax.axis_index("p")
    c_index = lax.axis_index("c")
    t_index = lax.axis_index(("x", "zh", "zl"))
    rows = ("c", "x", "zh", "zl")
    raw_txt = share(texts, "p").reshape(-1, width)
    both = lax.all_gather(images, "c", axis=0, tiled=True)
    n_img, n_txt = both.shape[0], raw_txt.shape[0]
    total = float(n_img * lax.axis_size("p"))
    img_ids = p_index * n_img + jnp.arange(n_img, dtype=jnp.int32)
    place = jnp.arange(n_txt, dtype=jnp.int32)
    txt_ids = t_index * (n_txt * CORES) + (place // own * CORES + c_index) * own + place % own
    both, img_ids, txt_ids = lax.optimization_barrier((both, img_ids, txt_ids))
    img_bf = normalize(both)[0].astype(jnp.bfloat16)
    txt_bf = normalize(raw_txt)[0].astype(jnp.bfloat16)
    scores = logit_scale * lax.dot_general(
        txt_bf, img_bf, (((1,), (1,)), ((), ())), preferred_element_type=jnp.float32
    )
    kernel = jnp.exp(scores - logit_scale)
    col_total = total_over(jnp.sum(kernel, axis=1), "p")
    col_sum = col_total
    for step in range(ROUNDS):
        col_scale = 1.0 / (total * col_sum)
        row_part = jnp.sum(kernel * col_scale[:, None], axis=0)
        if step == 0:
            stats = total_over(jnp.stack([row_part, jnp.sum(kernel, axis=0)]), rows)
            row_sum, row_total = stats[0], stats[1]
        else:
            row_sum = total_over(row_part, rows)
        row_weight = 1.0 / (total * row_sum)
        col_sum = total_over(jnp.sum(kernel * row_weight[None, :], axis=1), "p")
    col_weight = 1.0 - mix_weight + mix_weight * total * col_scale * col_sum
    by_row = 0.5 / row_total
    by_col = 0.5 * col_weight / col_total
    by_pair = mix_weight * total * row_weight
    same = txt_ids[:, None] == img_ids[None, :]
    grad_logit = kernel * (
        by_row[None, :] + by_col[:, None] - by_pair[None, :] * col_scale[:, None]
    ) - jnp.where(same, 1.0 - mix_weight, 0.0)
    grad_logit = grad_logit.astype(jnp.bfloat16)
    g_part = (
        logit_scale * jnp.dot(grad_logit, img_bf, preferred_element_type=jnp.float32)
    ).astype(jnp.bfloat16)
    g_part, grad_logit = lax.optimization_barrier((g_part, grad_logit))
    g_txt = scatter_sum(g_part.reshape(-1, own, width), "p")
    g_part = logit_scale * lax.dot_general(
        grad_logit, txt_bf, (((0,), (0,)), ((), ())), preferred_element_type=jnp.float32
    )
    g_part = keep_half(g_part, "c", 0, jnp.float32)
    g_part = g_part.reshape(NEAR, -1, width)
    g_part = keep_half(g_part, "zh", 1, jnp.bfloat16).astype(jnp.bfloat16)
    g_part, g_txt = lax.optimization_barrier((g_part, g_txt))
    g_img = scatter_sum(g_part.reshape(-1, own, width), ("x", "zl"))
    own_img = lax.dynamic_slice_in_dim(images, t_index * own, own, 0)
    grad_images = project_back(g_img, *normalize(own_img))
    grad_texts = project_back(g_txt, *normalize(texts))
    return (grad_images, grad_texts)


def solution(mesh):
    n_img, n_txt = mesh.devices.shape
    shape = (n_img // CORES, CORES, NEAR, FAR, n_txt // (NEAR * FAR))
    split = Mesh(mesh.devices.reshape(shape), ("p", "c", "x", "zh", "zl"))
    t = ("x", "zh", "zl")
    return jax.shard_map(
        shards,
        mesh=split,
        in_specs=(P(("p", "c"), None), P((*t, "p", "c"), None)),
        out_specs=(P(("p", "c", *t), None), P((*t, "p", "c"), None)),
        check_vma=False,
    )
```

```python
import jax
import jax.numpy as jnp
from jax import lax
from jax.sharding import Mesh, PartitionSpec as P

ROUNDS = 3
CORES = 2
NEAR = 2
FAR = 2

logit_scale = 30.0
mix_weight = 0.5
norm_eps = 1e-06


def normalize(values):
    wide = values.astype(jnp.float32)
    length = jnp.sqrt(jnp.sum(wide * wide, axis=1, keepdims=True) + norm_eps)
    return (wide / length, length)


def project_back(grad, unit, length):
    along = jnp.sum(unit * grad, axis=1, keepdims=True)
    return (grad - unit * along) / length


def exchange(parts, axes):
    return lax.all_to_all(parts, axes, 0, 0, tiled=True)


def share(values, axes):
    return exchange(jnp.broadcast_to(values[None], (lax.axis_size(axes),) + values.shape), axes)


def total_over(values, axes):
    return jnp.sum(share(values, axes), axis=0)


def scatter_sum(values, axes):
    return jnp.sum(exchange(values.astype(jnp.bfloat16), axes).astype(jnp.float32), axis=0)


def keep_half(values, start, axis, dim):
    half = values.shape[dim] // 2
    mine = take(values, start[0], half, dim)
    other = take(values, start[1], half, dim).astype(jnp.bfloat16)
    return mine + lax.ppermute(other, axis, [(0, 1), (1, 0)]).astype(jnp.float32)


def take(values, start, size, dim):
    starts = [jnp.uint32(0)] * values.ndim
    starts[dim] = start
    sizes = list(values.shape)
    sizes[dim] = size
    return lax.dynamic_slice(values, starts, sizes)


def shards(images, texts):
    own, width = texts.shape
    p_index = lax.axis_index("p")
    c_index = lax.axis_index("c")
    t_index = lax.axis_index(("x", "zh", "zl"))
    rows = ("c", "x", "zh", "zl")
    raw_txt = share(texts, "p").reshape(-1, width)
    both = lax.all_gather(images, "c", axis=0, tiled=True)
    n_img, n_txt = both.shape[0], raw_txt.shape[0]
    total = float(n_img * lax.axis_size("p"))
    img_ids = p_index * n_img + jnp.arange(n_img, dtype=jnp.int32)
    place = jnp.arange(n_txt, dtype=jnp.int32)
    txt_ids = t_index * (n_txt * CORES) + (place // own * CORES + c_index) * own + place % own
    half_c, half_z = n_img // 2, n_img // (2 * NEAR * FAR)
    z_index = lax.axis_index("zh")
    places = [c_index * half_c, (1 - c_index) * half_c, z_index * half_z, (1 - z_index) * half_z]
    places = [place.astype(jnp.uint32) for place in places]
    own_img = lax.dynamic_slice_in_dim(images, t_index * own, own, 0)
    own_units = normalize(own_img) + normalize(texts)
    both, img_ids, txt_ids, places, own_units = lax.optimization_barrier(
        (both, img_ids, txt_ids, places, own_units)
    )
    img_bf = normalize(both)[0].astype(jnp.bfloat16)
    txt_bf = normalize(raw_txt)[0].astype(jnp.bfloat16)
    scores = logit_scale * lax.dot_general(
        txt_bf, img_bf, (((1,), (1,)), ((), ())), preferred_element_type=jnp.float32
    )
    kernel = jnp.exp(scores - logit_scale)
    col_total = total_over(jnp.sum(kernel, axis=1), "p")
    col_sum = col_total
    for step in range(ROUNDS):
        col_scale = 1.0 / (total * col_sum)
        row_part = jnp.sum(kernel * col_scale[:, None], axis=0)
        if step == 0:
            stats = total_over(jnp.stack([row_part, jnp.sum(kernel, axis=0)]), rows)
            row_sum, row_total = stats[0], stats[1]
        else:
            row_sum = total_over(row_part, rows)
        row_weight = 1.0 / (total * row_sum)
        col_sum = total_over(jnp.sum(kernel * row_weight[None, :], axis=1), "p")
    col_weight = 1.0 - mix_weight + mix_weight * total * col_scale * col_sum
    by_row = 0.5 / row_total
    by_col = 0.5 * col_weight / col_total
    by_pair = mix_weight * total * row_weight
    same = txt_ids[:, None] == img_ids[None, :]
    grad_logit = kernel * (
        by_row[None, :] + by_col[:, None] - by_pair[None, :] * col_scale[:, None]
    ) - jnp.where(same, 1.0 - mix_weight, 0.0)
    grad_logit = grad_logit.astype(jnp.bfloat16)
    g_part = (
        logit_scale * jnp.dot(grad_logit, img_bf, preferred_element_type=jnp.float32)
    ).astype(jnp.bfloat16)
    g_part, grad_logit = lax.optimization_barrier((g_part, grad_logit))
    g_txt = scatter_sum(g_part.reshape(-1, own, width), "p")
    g_part = logit_scale * lax.dot_general(
        grad_logit, txt_bf, (((0,), (0,)), ((), ())), preferred_element_type=jnp.float32
    )
    g_part = keep_half(g_part, places[:2], "c", 0)
    g_part = g_part.reshape(NEAR, -1, width)
    g_part = keep_half(g_part, places[2:], "zh", 1).astype(jnp.bfloat16)
    g_part, g_txt = lax.optimization_barrier((g_part, g_txt))
    g_img = scatter_sum(g_part.reshape(-1, own, width), ("x", "zl"))
    grad_images = project_back(g_img, *own_units[:2])
    grad_texts = project_back(g_txt, *own_units[2:])
    return (grad_images, grad_texts)


def solution(mesh):
    n_img, n_txt = mesh.devices.shape
    shape = (n_img // CORES, CORES, NEAR, FAR, n_txt // (NEAR * FAR))
    split = Mesh(mesh.devices.reshape(shape), ("p", "c", "x", "zh", "zl"))
    t = ("x", "zh", "zl")
    return jax.shard_map(
        shards,
        mesh=split,
        in_specs=(P(("p", "c"), None), P((*t, "p", "c"), None)),
        out_specs=(P(("p", "c", *t), None), P((*t, "p", "c"), None)),
        check_vma=False,
    )
```

```python
import jax
import jax.numpy as jnp
from jax import lax
from jax.sharding import Mesh, PartitionSpec as P

ROUNDS = 3
CORES = 2
NEAR = 2
FAR = 2

logit_scale = 30.0
mix_weight = 0.5
norm_eps = 1e-06


def normalize(values):
    wide = values.astype(jnp.float32)
    length = jnp.sqrt(jnp.sum(wide * wide, axis=1, keepdims=True) + norm_eps)
    return (wide / length, length)


def project_back(grad, unit, length):
    along = jnp.sum(unit * grad, axis=1, keepdims=True)
    return (grad - unit * along) / length


def exchange(parts, axes):
    return lax.all_to_all(parts, axes, 0, 0, tiled=True)


def share(values, axes):
    return exchange(jnp.broadcast_to(values[None], (lax.axis_size(axes),) + values.shape), axes)


def total_over(values, axes):
    return jnp.sum(share(values, axes), axis=0)


def scatter_sum(values, axes):
    return jnp.sum(exchange(values.astype(jnp.bfloat16), axes).astype(jnp.float32), axis=0)


def keep_half(values, start, axis, dim):
    half = values.shape[dim] // 2
    mine = take(values, start[0], half, dim)
    other = take(values, start[1], half, dim).astype(jnp.bfloat16)
    return mine + lax.ppermute(other, axis, [(0, 1), (1, 0)]).astype(jnp.float32)


def take(values, start, size, dim):
    starts = [jnp.uint32(0)] * values.ndim
    starts[dim] = start
    sizes = list(values.shape)
    sizes[dim] = size
    return lax.dynamic_slice(values, starts, sizes)


def shards(images, texts):
    own, width = texts.shape
    p_index = lax.axis_index("p")
    c_index = lax.axis_index("c")
    t_index = lax.axis_index(("x", "zh", "zl"))
    rows = ("c", "x", "zh", "zl")
    raw_txt = share(texts, "p").reshape(-1, width)
    both = lax.all_gather(images, "c", axis=0, tiled=True)
    n_img, n_txt = both.shape[0], raw_txt.shape[0]
    total = float(n_img * lax.axis_size("p"))
    img_ids = p_index * n_img + jnp.arange(n_img, dtype=jnp.int32)
    place = jnp.arange(n_txt, dtype=jnp.int32)
    txt_ids = t_index * (n_txt * CORES) + (place // own * CORES + c_index) * own + place % own
    half_c, half_z = n_img // 2, n_img // (2 * NEAR * FAR)
    z_index = lax.axis_index("zh")
    places = [c_index * half_c, (1 - c_index) * half_c, z_index * half_z, (1 - z_index) * half_z]
    places = [place.astype(jnp.uint32) for place in places]
    own_img = lax.dynamic_slice_in_dim(images, t_index * own, own, 0)
    own_units = normalize(own_img) + normalize(texts)
    both, img_ids, txt_ids, places, own_units = lax.optimization_barrier(
        (both, img_ids, txt_ids, places, own_units)
    )
    img_bf = normalize(both)[0].astype(jnp.bfloat16)
    txt_bf = normalize(raw_txt)[0].astype(jnp.bfloat16)
    scores = logit_scale * lax.dot_general(
        txt_bf, img_bf, (((1,), (1,)), ((), ())), preferred_element_type=jnp.float32
    )
    kernel = jnp.exp(scores - logit_scale)
    col_total = total_over(jnp.sum(kernel, axis=1), "p")
    col_sum = col_total
    for step in range(ROUNDS):
        col_scale = 1.0 / (total * col_sum)
        row_part = jnp.sum(kernel * col_scale[:, None], axis=0)
        if step == 0:
            stats = total_over(jnp.stack([row_part, jnp.sum(kernel, axis=0)]), rows)
            row_sum, row_total = stats[0], stats[1]
        else:
            row_sum = total_over(row_part, rows)
        row_weight = 1.0 / (total * row_sum)
        col_sum = total_over(jnp.sum(kernel * row_weight[None, :], axis=1), "p")
    col_weight = 1.0 - mix_weight + mix_weight * total * col_scale * col_sum
    by_row = 0.5 / row_total
    by_col = 0.5 * col_weight / col_total
    by_pair = mix_weight * total * row_weight
    same = txt_ids[:, None] == img_ids[None, :]

    def logits(kernel):
        grad_logit = kernel * (
            by_row[None, :] + by_col[:, None] - by_pair[None, :] * col_scale[:, None]
        ) - jnp.where(same, 1.0 - mix_weight, 0.0)
        return grad_logit.astype(jnp.bfloat16)

    g_part = jnp.dot(logits(kernel), img_bf, preferred_element_type=jnp.float32)
    g_part, kernel = lax.optimization_barrier((g_part.astype(jnp.bfloat16), kernel))
    g_txt = logit_scale * scatter_sum(g_part.reshape(-1, own, width), "p")
    g_part = lax.dot_general(
        logits(kernel), txt_bf, (((0,), (0,)), ((), ())), preferred_element_type=jnp.float32
    )
    g_part = keep_half(g_part, places[:2], "c", 0)
    g_part = g_part.reshape(NEAR, -1, width)
    g_part = keep_half(g_part, places[2:], "zh", 1).astype(jnp.bfloat16)
    g_part, g_txt = lax.optimization_barrier((g_part, g_txt))
    g_img = logit_scale * scatter_sum(g_part.reshape(-1, own, width), ("x", "zl"))
    grad_images = project_back(g_img, *own_units[:2])
    grad_texts = project_back(g_txt, *own_units[2:])
    return (grad_images, grad_texts)


def solution(mesh):
    n_img, n_txt = mesh.devices.shape
    shape = (n_img // CORES, CORES, NEAR, FAR, n_txt // (NEAR * FAR))
    split = Mesh(mesh.devices.reshape(shape), ("p", "c", "x", "zh", "zl"))
    t = ("x", "zh", "zl")
    return jax.shard_map(
        shards,
        mesh=split,
        in_specs=(P(("p", "c"), None), P((*t, "p", "c"), None)),
        out_specs=(P(("p", "c", *t), None), P((*t, "p", "c"), None)),
        check_vma=False,
    )
```

```python
import jax
import jax.numpy as jnp
from jax import lax
from jax.experimental.layout import Layout, with_layout_constraint
from jax.sharding import Mesh, PartitionSpec as P

ROUNDS = 3
CORES = 2
NEAR = 2
FAR = 2

logit_scale = 30.0
mix_weight = 0.5
norm_eps = 1e-06


def normalize(values):
    wide = values.astype(jnp.float32)
    length = jnp.sqrt(jnp.sum(wide * wide, axis=1, keepdims=True) + norm_eps)
    return (wide / length, length)


def project_out(grad, unit):
    grad = with_layout_constraint(grad, Layout((0, 1)))
    return grad - unit * jnp.sum(unit * grad, axis=1, keepdims=True)


def exchange(parts, axes):
    return lax.all_to_all(parts, axes, 0, 0, tiled=True)


def share(values, axes):
    return exchange(jnp.broadcast_to(values[None], (lax.axis_size(axes),) + values.shape), axes)


def total_over(values, axes):
    return jnp.sum(share(values, axes), axis=0)


def scatter_sum(values, axes):
    return jnp.sum(exchange(values.astype(jnp.bfloat16), axes).astype(jnp.float32), axis=0)


def keep_half(values, start, axis, dim):
    half = values.shape[dim] // 2
    mine = take(values, start[0], half, dim)
    other = take(values, start[1], half, dim).astype(jnp.bfloat16)
    return mine + lax.ppermute(other, axis, [(0, 1), (1, 0)]).astype(jnp.float32)


def take(values, start, size, dim):
    starts = [jnp.uint32(0)] * values.ndim
    starts[dim] = start
    sizes = list(values.shape)
    sizes[dim] = size
    return lax.dynamic_slice(values, starts, sizes)


def shards(images, texts):
    own, width = texts.shape
    p_index = lax.axis_index("p")
    c_index = lax.axis_index("c")
    t_index = lax.axis_index(("x", "zh", "zl"))
    rows = ("c", "x", "zh", "zl")
    raw_txt = share(texts, "p").reshape(-1, width)
    both = lax.all_gather(images, "c", axis=0, tiled=True)
    n_img, n_txt = both.shape[0], raw_txt.shape[0]
    total = float(n_img * lax.axis_size("p"))
    img_ids = p_index * n_img + jnp.arange(n_img, dtype=jnp.int32)
    place = jnp.arange(n_txt, dtype=jnp.int32)
    txt_ids = t_index * (n_txt * CORES) + (place // own * CORES + c_index) * own + place % own
    half_c, half_z = n_img // 2, n_img // (2 * NEAR * FAR)
    z_index = lax.axis_index("zh")
    places = [c_index * half_c, (1 - c_index) * half_c, z_index * half_z, (1 - z_index) * half_z]
    places = [place.astype(jnp.uint32) for place in places]
    own_img = lax.dynamic_slice_in_dim(images, t_index * own, own, 0)
    lengths = (normalize(own_img)[1], normalize(texts)[1])
    both, img_ids, txt_ids, places, lengths = lax.optimization_barrier(
        (both, img_ids, txt_ids, places, lengths)
    )
    unit_img, unit_txt = normalize(both)[0], normalize(raw_txt)[0]
    img_bf, txt_bf = unit_img.astype(jnp.bfloat16), unit_txt.astype(jnp.bfloat16)
    scores = logit_scale * lax.dot_general(
        txt_bf, img_bf, (((1,), (1,)), ((), ())), preferred_element_type=jnp.float32
    )
    kernel = jnp.exp(scores - logit_scale)
    col_total = total_over(jnp.sum(kernel, axis=1), "p")
    col_sum = col_total
    for step in range(ROUNDS):
        col_scale = 1.0 / (total * col_sum)
        row_part = jnp.sum(kernel * col_scale[:, None], axis=0)
        if step == 0:
            stats = total_over(jnp.stack([row_part, jnp.sum(kernel, axis=0)]), rows)
            row_sum, row_total = stats[0], stats[1]
        else:
            row_sum = total_over(row_part, rows)
        row_weight = 1.0 / (total * row_sum)
        col_sum = total_over(jnp.sum(kernel * row_weight[None, :], axis=1), "p")
    col_weight = 1.0 - mix_weight + mix_weight * total * col_scale * col_sum
    by_row = 0.5 / row_total
    by_col = 0.5 * col_weight / col_total
    by_pair = mix_weight * total * row_weight
    same = txt_ids[:, None] == img_ids[None, :]

    def logits(kernel):
        grad_logit = kernel * (
            by_row[None, :] + by_col[:, None] - by_pair[None, :] * col_scale[:, None]
        ) - jnp.where(same, 1.0 - mix_weight, 0.0)
        return grad_logit.astype(jnp.bfloat16)

    g_part = jnp.dot(logits(kernel), img_bf, preferred_element_type=jnp.float32)
    g_part = project_out(g_part, unit_txt)
    g_part, kernel = lax.optimization_barrier((g_part.astype(jnp.bfloat16), kernel))
    g_txt = logit_scale * scatter_sum(g_part.reshape(-1, own, width), "p")
    g_part = lax.dot_general(
        logits(kernel), txt_bf, (((0,), (0,)), ((), ())), preferred_element_type=jnp.float32
    )
    g_part = project_out(g_part, unit_img)
    g_part = keep_half(g_part, places[:2], "c", 0)
    g_part = g_part.reshape(NEAR, -1, width)
    g_part = keep_half(g_part, places[2:], "zh", 1).astype(jnp.bfloat16)
    g_part, g_txt = lax.optimization_barrier((g_part, g_txt))
    g_img = logit_scale * scatter_sum(g_part.reshape(-1, own, width), ("x", "zl"))
    grad_images = g_img / lengths[0]
    grad_texts = g_txt / lengths[1]
    return (grad_images, grad_texts)


def solution(mesh):
    n_img, n_txt = mesh.devices.shape
    shape = (n_img // CORES, CORES, NEAR, FAR, n_txt // (NEAR * FAR))
    split = Mesh(mesh.devices.reshape(shape), ("p", "c", "x", "zh", "zl"))
    t = ("x", "zh", "zl")
    return jax.shard_map(
        shards,
        mesh=split,
        in_specs=(P(("p", "c"), None), P((*t, "p", "c"), None)),
        out_specs=(P(("p", "c", *t), None), P((*t, "p", "c"), None)),
        check_vma=False,
    )
```

```python
import jax
import jax.numpy as jnp
from jax import lax
from jax.experimental.layout import Layout, with_layout_constraint
from jax.sharding import Mesh, PartitionSpec as P

ROUNDS = 3
CORES = 2
NEAR = 2
FAR = 2

logit_scale = 30.0
mix_weight = 0.5
norm_eps = 1e-06


def normalize(values):
    wide = values.astype(jnp.float32)
    length = jnp.sqrt(jnp.sum(wide * wide, axis=1, keepdims=True) + norm_eps)
    return (wide / length, length)


def project_out(grad, unit):
    grad = with_layout_constraint(grad, Layout((0, 1)))
    return grad - unit * jnp.sum(unit * grad, axis=1, keepdims=True)


def exchange(parts, axes):
    return lax.all_to_all(parts, axes, 0, 0, tiled=True)


def share(values, axes):
    return exchange(jnp.broadcast_to(values[None], (lax.axis_size(axes),) + values.shape), axes)


def total_over(values, axes):
    return jnp.sum(share(values, axes), axis=0)


def scatter_sum(values, axes):
    return jnp.sum(exchange(values.astype(jnp.bfloat16), axes).astype(jnp.float32), axis=0)


def keep_half(values, start, axis, dim):
    half = values.shape[dim] // 2
    mine = take(values, start[0], half, dim)
    other = take(values, start[1], half, dim).astype(jnp.bfloat16)
    return mine + lax.ppermute(other, axis, [(0, 1), (1, 0)]).astype(jnp.float32)


def take(values, start, size, dim):
    starts = [jnp.uint32(0)] * values.ndim
    starts[dim] = start
    sizes = list(values.shape)
    sizes[dim] = size
    return lax.dynamic_slice(values, starts, sizes)


def shards(images, texts):
    own, width = texts.shape
    p_index = lax.axis_index("p")
    c_index = lax.axis_index("c")
    t_index = lax.axis_index(("x", "zh", "zl"))
    rows = ("c", "x", "zh", "zl")
    raw_txt = share(texts, "p").reshape(-1, width)
    both = lax.all_gather(images, "c", axis=0, tiled=True)
    n_img, n_txt = both.shape[0], raw_txt.shape[0]
    total = float(n_img * lax.axis_size("p"))
    img_ids = p_index * n_img + jnp.arange(n_img, dtype=jnp.int32)
    place = jnp.arange(n_txt, dtype=jnp.int32)
    txt_ids = t_index * (n_txt * CORES) + (place // own * CORES + c_index) * own + place % own
    half_c, half_z = n_img // 2, n_img // (2 * NEAR * FAR)
    z_index = lax.axis_index("zh")
    places = [c_index * half_c, (1 - c_index) * half_c, z_index * half_z, (1 - z_index) * half_z]
    places = [place.astype(jnp.uint32) for place in places]
    own_img = lax.dynamic_slice_in_dim(images, t_index * own, own, 0)
    lengths = (normalize(own_img)[1], normalize(texts)[1])
    both, img_ids, txt_ids, places, lengths = lax.optimization_barrier(
        (both, img_ids, txt_ids, places, lengths)
    )
    unit_img, len_img = normalize(both)
    unit_txt, len_txt = normalize(raw_txt)
    img_bf, txt_bf = unit_img.astype(jnp.bfloat16), unit_txt.astype(jnp.bfloat16)
    scores = logit_scale * lax.dot_general(
        txt_bf, img_bf, (((1,), (1,)), ((), ())), preferred_element_type=jnp.float32
    )
    kernel = jnp.exp(scores - logit_scale)
    col_total = total_over(jnp.sum(kernel, axis=1), "p")
    col_sum = col_total
    for step in range(ROUNDS):
        col_scale = 1.0 / (total * col_sum)
        row_part = jnp.sum(kernel * col_scale[:, None], axis=0)
        if step == 0:
            stats = total_over(jnp.stack([row_part, jnp.sum(kernel, axis=0)]), rows)
            row_sum, row_total = stats[0], stats[1]
        else:
            row_sum = total_over(row_part, rows)
        row_weight = 1.0 / (total * row_sum)
        col_sum = total_over(jnp.sum(kernel * row_weight[None, :], axis=1), "p")
    kept = (both, len_img, raw_txt, len_txt, row_weight)
    both, len_img, raw_txt, len_txt, row_weight = lax.optimization_barrier(kept)
    unit_img, unit_txt = both.astype(jnp.float32) / len_img, raw_txt.astype(jnp.float32) / len_txt
    col_weight = 1.0 - mix_weight + mix_weight * total * col_scale * col_sum
    by_row = 0.5 / row_total
    by_col = 0.5 * col_weight / col_total
    by_pair = mix_weight * total * row_weight
    same = txt_ids[:, None] == img_ids[None, :]

    def logits(kernel):
        grad_logit = kernel * (
            by_row[None, :] + by_col[:, None] - by_pair[None, :] * col_scale[:, None]
        ) - jnp.where(same, 1.0 - mix_weight, 0.0)
        return grad_logit.astype(jnp.bfloat16)

    g_part = jnp.dot(logits(kernel), img_bf, preferred_element_type=jnp.float32)
    g_part = project_out(g_part, unit_txt)
    g_part, kernel = lax.optimization_barrier((g_part.astype(jnp.bfloat16), kernel))
    g_txt = logit_scale * scatter_sum(g_part.reshape(-1, own, width), "p")
    g_part = lax.dot_general(
        logits(kernel), txt_bf, (((0,), (0,)), ((), ())), preferred_element_type=jnp.float32
    )
    g_part = project_out(g_part, unit_img)
    g_part = keep_half(g_part, places[:2], "c", 0)
    g_part = g_part.reshape(NEAR, -1, width)
    g_part = keep_half(g_part, places[2:], "zh", 1).astype(jnp.bfloat16)
    g_part, g_txt = lax.optimization_barrier((g_part, g_txt))
    g_img = logit_scale * scatter_sum(g_part.reshape(-1, own, width), ("x", "zl"))
    grad_images = g_img / lengths[0]
    grad_texts = g_txt / lengths[1]
    return (grad_images, grad_texts)


def solution(mesh):
    n_img, n_txt = mesh.devices.shape
    shape = (n_img // CORES, CORES, NEAR, FAR, n_txt // (NEAR * FAR))
    split = Mesh(mesh.devices.reshape(shape), ("p", "c", "x", "zh", "zl"))
    t = ("x", "zh", "zl")
    return jax.shard_map(
        shards,
        mesh=split,
        in_specs=(P(("p", "c"), None), P((*t, "p", "c"), None)),
        out_specs=(P(("p", "c", *t), None), P((*t, "p", "c"), None)),
        check_vma=False,
    )
```
